32 devices in a mesh: fsdp: 16 (over z, y, core), ctx: 2 (over x).
Axes of the slice: x: 2, y: 2, z: 4, core: 2. Of those that a mesh axis runs over, the one named last changes fastest.
Arguments:
- tokens: bfloat16 [4096, 1024], P(('fsdp', 'ctx')), may hold values from -6 to 6
- cotangent: bfloat16 [4096, 1024], P(('fsdp', 'ctx')), may hold values from -6 to 6
- seq_lengths: int32 [16, 4], P('fsdp'), may hold values from 1 to 128, 256 in all within a row
- query_key_value_weight: float32 [1024, 4096], P(('fsdp', 'ctx')), may hold values from -0.1875 to 0.1875
- first_moment_projection: float32 [1024, 4096], P(('fsdp', 'ctx')), may hold values from -12 to 12
- second_moment_projection: float32 [1024, 4096], P(('fsdp', 'ctx')), may hold values from 1 to 100
- w_out: float32 [2048, 1024], P(('fsdp', 'ctx')), may hold values from -0.625 to 0.625
- m_out: float32 [2048, 1024], P(('fsdp', 'ctx')), may hold values from -12 to 12
- v_out: float32 [2048, 1024], P(('fsdp', 'ctx')), may hold values from 1 to 100
- w_gateup: float32 [1024, 6144], P(('fsdp', 'ctx')), may hold values from -0.1875 to 0.1875
- m_gateup: float32 [1024, 6144], P(('fsdp', 'ctx')), may hold values from -12 to 12
- v_gateup: float32 [1024, 6144], P(('fsdp', 'ctx')), may hold values from 1 to 100
- w_down: float32 [3072, 1024], P(('fsdp', 'ctx')), may hold values from -0.109375 to 0.109375
- m_down: float32 [3072, 1024], P(('fsdp', 'ctx')), may hold values from -12 to 12
- v_down: float32 [3072, 1024], P(('fsdp', 'ctx')), may hold values from 1 to 100
- attn_gain: float32 [1024], replicated, may hold values from 0.5 to 1.5
- m_attn_gain: float32 [1024], replicated, may hold values from -120 to 120
- v_attn_gain: float32 [1024], replicated, may hold values from 100 to 10000
- mlp_gain: float32 [1024], replicated, may hold values from 0.5 to 1.5
- m_mlp_gain: float32 [1024], replicated, may hold values from -120 to 120
- v_mlp_gain: float32 [1024], replicated, may hold values from 100 to 10000
- q_gain: float32 [128], replicated, may hold values from 0.5 to 1.5
- m_q_gain: float32 [128], replicated, may hold values from -120 to 120
- v_q_gain: float32 [128], replicated, may hold values from 100 to 10000
- k_gain: float32 [128], replicated, may hold values from 0.5 to 1.5
- m_k_gain: float32 [128], replicated, may hold values from -120 to 120
- v_k_gain: float32 [128], replicated, may hold values from 100 to 10000
Outputs:
- output: bfloat16 [4096, 1024], P(('fsdp', 'ctx'))
- grad_tokens: float32 [4096, 1024], P(('fsdp', 'ctx'))
- grad_qkv: float32 [1024, 4096], P(('fsdp', 'ctx'))
- new_w_qkv: float32 [1024, 4096], P(('fsdp', 'ctx'))
- new_m_qkv: float32 [1024, 4096], P(('fsdp', 'ctx'))
- new_v_qkv: float32 [1024, 4096], P(('fsdp', 'ctx'))
- grad_out: float32 [2048, 1024], P(('fsdp', 'ctx'))
- new_w_out: float32 [2048, 1024], P(('fsdp', 'ctx'))
- new_m_out: float32 [2048, 1024], P(('fsdp', 'ctx'))
- new_v_out: float32 [2048, 1024], P(('fsdp', 'ctx'))
- grad_gateup: float32 [1024, 6144], P(('fsdp', 'ctx'))
- new_w_gateup: float32 [1024, 6144], P(('fsdp', 'ctx'))
- new_m_gateup: float32 [1024, 6144], P(('fsdp', 'ctx'))
- new_v_gateup: float32 [1024, 6144], P(('fsdp', 'ctx'))
- grad_down: float32 [3072, 1024], P(('fsdp', 'ctx'))
- new_w_down: float32 [3072, 1024], P(('fsdp', 'ctx'))
- new_m_down: float32 [3072, 1024], P(('fsdp', 'ctx'))
- new_v_down: float32 [3072, 1024], P(('fsdp', 'ctx'))
- grad_attn_gain: float32 [1024], replicated
- new_attn_gain: float32 [1024], replicated
- new_m_attn_gain: float32 [1024], replicated
- new_v_attn_gain: float32 [1024], replicated
- grad_mlp_gain: float32 [1024], replicated
- new_mlp_gain: float32 [1024], replicated
- new_m_mlp_gain: float32 [1024], replicated
- new_v_mlp_gain: float32 [1024], replicated
- grad_q_gain: float32 [128], replicated
- new_q_gain: float32 [128], replicated
- new_m_q_gain: float32 [128], replicated
- new_v_q_gain: float32 [128], replicated
- grad_k_gain: float32 [128], replicated
- new_k_gain: float32 [128], replicated
- new_m_k_gain: float32 [128], replicated
- new_v_k_gain: float32 [128], replicated
The draws below stay inside these ranges and needn't reach their ends.
Inputs may be any that keep to these rules, and one draw needn't show every extreme that they name: `seq_lengths`: each row holds the lengths of the 4 sequences packed one after another into a group; a row sums to 256 and its largest entry is exactly 128.
All inputs are finite; a program needn't handle non-finite values.
Results may differ from the reference program's by a relative error of at most 0.025.
Values may be sent and summed in bfloat16 or wider, within the bound.
No kernel may reach another device: no remote copies, remote signals or barrier semaphores. Data moves between devices by JAX's collectives and lax.ppermute only.
A program may use at most 256 MiB of HBM per device.

```python
import math
import jax
import jax.numpy as jnp
import numpy as np
from jax import lax

MODEL_WIDTH = 1024
QUERY_HEADS = 16
KEY_VALUE_HEADS = 8
HEAD_WIDTH = 128
FF = 3072
TOK_DEV = 128
SEQS = 4
STEP = 3
TOK_GROUP = 256
MAX_LEN = 128
TOKENS = 4096
N_FSDP = 16
N_CTX = 2


def level_of(key, extent, shards, smallest, top_value):
    def one(dim, blocks):
        draws = jax.random.uniform(jax.random.fold_in(jax.random.fold_in(key, 6), dim), (blocks,), jnp.float32, smallest / len(shards), top_value / len(shards))
        return jnp.repeat(jnp.exp(draws), extent[dim] // blocks).reshape((-1,) + (1,) * (len(extent) - dim - 1))

    level = one(*shards[0])
    for cut in shards[1:]:
        level = level * one(*cut)
    return level


def length_profile(amount, total, limit, skew):
    loads = [(1 << 20) // math.isqrt(standing ** skew) + 1 for standing in range(2, amount + 1)]
    rest, holding = total - limit - (amount - 1), [1] * (amount - 1)
    while rest > 0:
        movable = [i for i in range(amount - 1) if holding[i] < limit]
        pool, budget = sum([loads[i] for i in movable]), rest
        for i in movable:
            addition = min(limit - holding[i], max(1, budget * loads[i] // pool), rest)
            holding[i] = holding[i] + addition
            rest = rest - addition
    return np.array([limit] + holding)


def ragged(own_key, number_of, total, reach, skew):
    if number_of == 2:
        one = jax.random.randint(own_key, (), max(1, total - reach), min(reach, total - 1) + 1)
        return jnp.stack([one, total - one])
    sizes = jnp.asarray(length_profile(number_of, total, reach, skew), jnp.int32)
    pairs = (number_of - 1) // 2
    donor, sink = sizes[1:1 + 2 * pairs:2], sizes[2:2 + 2 * pairs:2]
    slack = jnp.minimum(donor - 1, reach - sink)
    moved = jax.random.randint(jax.random.fold_in(own_key, 1), (pairs,), 0, 1 << 20) % (slack + 1)
    sizes = sizes.at[1:1 + 2 * pairs:2].set(donor - moved).at[2:2 + 2 * pairs:2].set(sink + moved)
    return sizes[jax.random.permutation(jax.random.fold_in(own_key, 2), number_of)]


def normal_values(own_key, dims, spread, limit, shards=(), kind=jnp.bfloat16):
    array = spread * jax.random.normal(own_key, dims, jnp.float32)
    if shards:
        array = array * level_of(own_key, dims, shards, -0.22, 0.18)
    return jnp.clip(array, -limit, limit).astype(kind)


def setup_inputs(seed: int = 0) -> dict:
    splits = jax.random.split(jax.random.key(seed), 28)
    return {
        "tokens": normal_values(splits[0], (TOKENS, MODEL_WIDTH), 1.0, 6.0, ((0, 32),)),
        "cotangent": normal_values(splits[1], (TOKENS, MODEL_WIDTH), 1.0, 6.0, ((0, 32),)),
        "seq_lengths": jax.vmap(lambda own: ragged(own, SEQS, TOK_GROUP, MAX_LEN, 2))(jax.random.split(splits[2], N_FSDP)).reshape((N_FSDP, SEQS)).astype(jnp.int32),
        "query_key_value_weight": normal_values(splits[3], (MODEL_WIDTH, (QUERY_HEADS + 2 * KEY_VALUE_HEADS) * HEAD_WIDTH), MODEL_WIDTH ** -0.5, 0.1875, ((0, 32),), jnp.float32),
        "first_moment_projection": normal_values(splits[4], (MODEL_WIDTH, (QUERY_HEADS + 2 * KEY_VALUE_HEADS) * HEAD_WIDTH), 2.0, 12.0, ((0, 32),), jnp.float32),
        "second_moment_projection": jnp.clip(jnp.exp(math.log(100.0) - 4.6051702 * jax.random.uniform(splits[5], (MODEL_WIDTH, (QUERY_HEADS + 2 * KEY_VALUE_HEADS) * HEAD_WIDTH), jnp.float32) ** level_of(splits[5], (MODEL_WIDTH, (QUERY_HEADS + 2 * KEY_VALUE_HEADS) * HEAD_WIDTH), ((0, 32),), -0.2, 0.2)), 1.0, 100.0),
        "w_out": normal_values(splits[6], (QUERY_HEADS * HEAD_WIDTH, MODEL_WIDTH), (QUERY_HEADS * HEAD_WIDTH * 6 // MAX_LEN) ** -0.5, 0.625, ((0, 32),), jnp.float32),
        "m_out": normal_values(splits[7], (QUERY_HEADS * HEAD_WIDTH, MODEL_WIDTH), 2.0, 12.0, ((0, 32),), jnp.float32),
        "v_out": jnp.clip(jnp.exp(math.log(100.0) - 4.6051702 * jax.random.uniform(splits[8], (QUERY_HEADS * HEAD_WIDTH, MODEL_WIDTH), jnp.float32) ** level_of(splits[8], (QUERY_HEADS * HEAD_WIDTH, MODEL_WIDTH), ((0, 32),), -0.2, 0.2)), 1.0, 100.0),
        "w_gateup": normal_values(splits[9], (MODEL_WIDTH, 2 * FF), MODEL_WIDTH ** -0.5, 0.1875, ((0, 32),), jnp.float32),
        "m_gateup": normal_values(splits[10], (MODEL_WIDTH, 2 * FF), 2.0, 12.0, ((0, 32),), jnp.float32),
        "v_gateup": jnp.clip(jnp.exp(math.log(100.0) - 4.6051702 * jax.random.uniform(splits[11], (MODEL_WIDTH, 2 * FF), jnp.float32) ** level_of(splits[11], (MODEL_WIDTH, 2 * FF), ((0, 32),), -0.2, 0.2)), 1.0, 100.0),
        "w_down": normal_values(splits[12], (FF, MODEL_WIDTH), FF ** -0.5, 0.109375, ((0, 32),), jnp.float32),
        "m_down": normal_values(splits[13], (FF, MODEL_WIDTH), 2.0, 12.0, ((0, 32),), jnp.float32),
        "v_down": jnp.clip(jnp.exp(math.log(100.0) - 4.6051702 * jax.random.uniform(splits[14], (FF, MODEL_WIDTH), jnp.float32) ** level_of(splits[14], (FF, MODEL_WIDTH), ((0, 32),), -0.2, 0.2)), 1.0, 100.0),
        "attn_gain": jnp.clip(1.0 + 0.1 * jax.random.normal(splits[15], (MODEL_WIDTH,), jnp.float32), 0.5, 1.5),
        "m_attn_gain": normal_values(splits[16], (MODEL_WIDTH,), 20.0, 120.0, (), jnp.float32),
        "v_attn_gain": jnp.clip(jnp.exp(jax.random.uniform(splits[17], (MODEL_WIDTH,), jnp.float32, math.log(100.0), math.log(10000.0))), 100.0, 10000.0),
        "mlp_gain": jnp.clip(1.0 + 0.1 * jax.random.normal(splits[18], (MODEL_WIDTH,), jnp.float32), 0.5, 1.5),
        "m_mlp_gain": normal_values(splits[19], (MODEL_WIDTH,), 20.0, 120.0, (), jnp.float32),
        "v_mlp_gain": jnp.clip(jnp.exp(jax.random.uniform(splits[20], (MODEL_WIDTH,), jnp.float32, math.log(100.0), math.log(10000.0))), 100.0, 10000.0),
        "q_gain": jnp.clip(1.0 + 0.1 * jax.random.normal(splits[21], (HEAD_WIDTH,), jnp.float32), 0.5, 1.5),
        "m_q_gain": normal_values(splits[22], (HEAD_WIDTH,), 20.0, 120.0, (), jnp.float32),
        "v_q_gain": jnp.clip(jnp.exp(jax.random.uniform(splits[23], (HEAD_WIDTH,), jnp.float32, math.log(100.0), math.log(10000.0))), 100.0, 10000.0),
        "k_gain": jnp.clip(1.0 + 0.1 * jax.random.normal(splits[24], (HEAD_WIDTH,), jnp.float32), 0.5, 1.5),
        "m_k_gain": normal_values(splits[25], (HEAD_WIDTH,), 20.0, 120.0, (), jnp.float32),
        "v_k_gain": jnp.clip(jnp.exp(jax.random.uniform(splits[26], (HEAD_WIDTH,), jnp.float32, math.log(100.0), math.log(10000.0))), 100.0, 10000.0),
    }


NORM_EPS = 1e-06
ROPE_BASE = 1000000.0
NEG_LARGE = -1e+30
BETA_ONE = 0.9
BETA_TWO = 0.95
ADAM_EPS = 1e-08
MATRIX_RATE = 0.04
GAIN_RATE = 0.2
MATRIX_DECAY = 0.1

def seq_place(lengths, positions):
    ends = jnp.cumsum(lengths).astype(jnp.int32)
    passed = ends[None, :] <= positions[:, None]
    segment = lax.optimization_barrier(jnp.sum(passed.astype(jnp.int32), axis=1)).astype(jnp.int32)
    start = lax.optimization_barrier(jnp.sum(jnp.where(passed, lengths[None, :], 0), axis=1)).astype(jnp.int32)
    return (segment, (positions - start).astype(jnp.int32))

def rope_tables(offsets, head_size):
    half_size = head_size // 2
    freqs = ROPE_BASE ** (-(2.0 * jnp.arange(half_size, dtype=jnp.float32)) / head_size)
    angles = offsets.astype(jnp.float32)[:, None] * freqs[None, :]
    cosine = jnp.concatenate([jnp.cos(angles), jnp.cos(angles)], axis=1)[:, None, :]
    sine = jnp.concatenate([jnp.sin(angles), jnp.sin(angles)], axis=1)[:, None, :]
    return (cosine, sine)

def rope_apply(values, cosine, sine):
    half_size = values.shape[-1] // 2
    rotated = jnp.concatenate([-values[..., half_size:], values[..., :half_size]], axis=-1)
    return values * cosine + rotated * sine

def rope_back(grads, cosine, sine):
    half_size = grads.shape[-1] // 2
    scaled = grads * sine
    return grads * cosine + jnp.concatenate([scaled[..., half_size:], -scaled[..., :half_size]], axis=-1)

def norm_back(grads, values, inv_rms, gain):
    scaled = grads * gain
    return inv_rms * scaled - values * (inv_rms * inv_rms * inv_rms) * lax.optimization_barrier(jnp.mean(scaled * values, axis=-1, keepdims=True))

def adamw(weight, first, second, grads, rate, decay):
    new_first = BETA_ONE * first + (1.0 - BETA_ONE) * grads
    new_second = BETA_TWO * second + (1.0 - BETA_TWO) * grads * grads
    first_hat = new_first / (1.0 - BETA_ONE ** STEP)
    second_hat = new_second / (1.0 - BETA_TWO ** STEP)
    new_weight = weight - rate * (first_hat / (jnp.sqrt(second_hat) + ADAM_EPS) + decay * weight)
    return (new_weight, new_first, new_second)

def f32_einsum(form, left, right):
    return jnp.einsum(form, left.astype(jnp.float32), right.astype(jnp.float32), precision=lax.Precision.HIGHEST)

def reference(tokens, cotangent, seq_lengths, query_key_value_weight, first_moment_projection, second_moment_projection, w_out, m_out, v_out, w_gateup, m_gateup, v_gateup, w_down, m_down, v_down, attn_gain, m_attn_gain, v_attn_gain, mlp_gain, m_mlp_gain, v_mlp_gain, q_gain, m_q_gain, v_q_gain, k_gain, m_k_gain, v_k_gain):
    grouped_rows = TOK_DEV * N_CTX
    heads_per_group = QUERY_HEADS // KEY_VALUE_HEADS
    key_value_width = KEY_VALUE_HEADS * HEAD_WIDTH
    score_scale = 1.0 / math.sqrt(HEAD_WIDTH)
    qkv_half = query_key_value_weight.astype(jnp.bfloat16)
    out_half = w_out.astype(jnp.bfloat16)
    gateup_half = w_gateup.astype(jnp.bfloat16)
    down_half = w_down.astype(jnp.bfloat16)

    def group_step(carry, inputs):
        tok_block, cot_block, lengths = inputs
        places = jnp.arange(grouped_rows, dtype=jnp.int32)
        segment, offsets = seq_place(lengths, places)
        allowed = (segment[:, None] == segment[None, :]) & (places[None, :] <= places[:, None])
        cosine, sine = rope_tables(offsets, HEAD_WIDTH)
        tok_float = tok_block.astype(jnp.float32)
        inv_one = lax.rsqrt(lax.optimization_barrier(jnp.mean(tok_float * tok_float, axis=1, keepdims=True)) + NORM_EPS)
        normed_one = (tok_float * inv_one * attn_gain).astype(jnp.bfloat16)
        projected_rows = jnp.dot(normed_one, qkv_half, preferred_element_type=jnp.float32)
        query = projected_rows[:, :QUERY_HEADS * HEAD_WIDTH].reshape(grouped_rows, QUERY_HEADS, HEAD_WIDTH)
        unrotated_key = projected_rows[:, QUERY_HEADS * HEAD_WIDTH:QUERY_HEADS * HEAD_WIDTH + key_value_width].reshape(grouped_rows, KEY_VALUE_HEADS, HEAD_WIDTH)
        unprojected_value = projected_rows[:, QUERY_HEADS * HEAD_WIDTH + key_value_width:]
        inv_q = lax.rsqrt(lax.optimization_barrier(jnp.mean(query * query, axis=2, keepdims=True)) + NORM_EPS)
        inv_k = lax.rsqrt(lax.optimization_barrier(jnp.mean(unrotated_key * unrotated_key, axis=2, keepdims=True)) + NORM_EPS)
        rotated_query = rope_apply(query * inv_q * q_gain, cosine, sine).astype(jnp.bfloat16)
        k_rot = rope_apply(unrotated_key * inv_k * k_gain, cosine, sine).astype(jnp.bfloat16)
        value_halfwidth = unprojected_value.astype(jnp.bfloat16).reshape(grouped_rows, KEY_VALUE_HEADS, HEAD_WIDTH)
        query_four_dims = rotated_query.reshape(grouped_rows, KEY_VALUE_HEADS, heads_per_group, HEAD_WIDTH)
        scores = f32_einsum('tkgd,jkd->kgtj', query_four_dims, k_rot) * score_scale
        scores = jnp.where(allowed, scores, NEG_LARGE)
        peak = lax.optimization_barrier(jnp.max(scores, axis=3, keepdims=True))
        expd = jnp.exp(scores - peak)
        totals = lax.optimization_barrier(jnp.sum(expd, axis=3, keepdims=True))
        log_total = peak + jnp.log(totals)
        probs_half = jnp.exp(scores - log_total).astype(jnp.bfloat16)
        attn_half = f32_einsum('kgtj,jkd->tkgd', probs_half, value_halfwidth).reshape(grouped_rows, QUERY_HEADS * HEAD_WIDTH).astype(jnp.bfloat16)
        resid = tok_float + jnp.dot(attn_half, out_half, preferred_element_type=jnp.float32)
        inv_two = lax.rsqrt(lax.optimization_barrier(jnp.mean(resid * resid, axis=1, keepdims=True)) + NORM_EPS)
        normed_two = (resid * inv_two * mlp_gain).astype(jnp.bfloat16)
        gate_up = jnp.dot(normed_two, gateup_half, preferred_element_type=jnp.float32)
        gate = gate_up[:, :FF]
        upper = gate_up[:, FF:]
        sigm = jax.nn.sigmoid(gate)
        active = gate * sigm
        hidden = (active * upper).astype(jnp.bfloat16)
        output = (resid + jnp.dot(hidden, down_half, preferred_element_type=jnp.float32)).astype(jnp.bfloat16)
        grad_down = jnp.dot(hidden.T, cot_block, preferred_element_type=jnp.float32)
        grad_hidden = jnp.dot(cot_block, down_half.T, preferred_element_type=jnp.float32)
        grad_gate = grad_hidden * upper * (sigm * (1.0 + gate * (1.0 - sigm)))
        grad_upper = grad_hidden * active
        grad_gu = jnp.concatenate([grad_gate, grad_upper], axis=1).astype(jnp.bfloat16)
        grad_gateup = jnp.dot(normed_two.T, grad_gu, preferred_element_type=jnp.float32)
        grad_n_two = jnp.dot(grad_gu, gateup_half.T, preferred_element_type=jnp.float32)
        gain_two = lax.optimization_barrier(jnp.sum(grad_n_two * resid * inv_two, axis=0))
        grad_resid = cot_block.astype(jnp.float32) + norm_back(grad_n_two, resid, inv_two, mlp_gain)
        resid_half = grad_resid.astype(jnp.bfloat16)
        grad_out = jnp.dot(attn_half.T, resid_half, preferred_element_type=jnp.float32)
        attention_gradient = jnp.dot(resid_half, out_half.T, preferred_element_type=jnp.float32).astype(jnp.bfloat16)
        attention_gradient = attention_gradient.reshape(grouped_rows, KEY_VALUE_HEADS, heads_per_group, HEAD_WIDTH)
        grad_probs = f32_einsum('tkgd,jkd->kgtj', attention_gradient, value_halfwidth)
        probs_full = jnp.exp(scores - log_total)
        grad_scores = probs_full * (grad_probs - lax.optimization_barrier(jnp.sum(probs_full * grad_probs, axis=3, keepdims=True)))
        scores_half = (grad_scores * score_scale).astype(jnp.bfloat16)
        grad_qrot = f32_einsum('kgtj,jkd->tkgd', scores_half, k_rot).reshape(grouped_rows, QUERY_HEADS, HEAD_WIDTH)
        rotated_key_gradient = f32_einsum('kgtj,tkgd->jkd', scores_half, query_four_dims)
        grad_value = f32_einsum('kgtj,tkgd->jkd', probs_half, attention_gradient).reshape(grouped_rows, key_value_width)
        grad_qn = rope_back(grad_qrot, cosine, sine)
        grad_kn = rope_back(rotated_key_gradient, cosine, sine)
        gain_q = lax.optimization_barrier(jnp.sum(grad_qn * query * inv_q, axis=(0, 1)))
        gain_k = lax.optimization_barrier(jnp.sum(grad_kn * unrotated_key * inv_k, axis=(0, 1)))
        grad_query = norm_back(grad_qn, query, inv_q, q_gain).reshape(grouped_rows, QUERY_HEADS * HEAD_WIDTH)
        grad_key = norm_back(grad_kn, unrotated_key, inv_k, k_gain).reshape(grouped_rows, key_value_width)
        grad_proj = jnp.concatenate([grad_query, grad_key, grad_value], axis=1).astype(jnp.bfloat16)
        grad_qkv = jnp.dot(normed_one.T, grad_proj, preferred_element_type=jnp.float32)
        grad_n_one = jnp.dot(grad_proj, qkv_half.T, preferred_element_type=jnp.float32)
        gain_one = lax.optimization_barrier(jnp.sum(grad_n_one * tok_float * inv_one, axis=0))
        grad_tokens = grad_resid + norm_back(grad_n_one, tok_float, inv_one, attn_gain)
        terms = (grad_qkv, grad_out, grad_gateup, grad_down, gain_one, gain_two, gain_q, gain_k)
        new_carry = tuple((held + term for held, term in zip(carry, terms)))
        return (new_carry, (output, grad_tokens))
    init = (jnp.zeros(query_key_value_weight.shape, jnp.float32), jnp.zeros(w_out.shape, jnp.float32), jnp.zeros(w_gateup.shape, jnp.float32), jnp.zeros(w_down.shape, jnp.float32), jnp.zeros((MODEL_WIDTH,), jnp.float32), jnp.zeros((MODEL_WIDTH,), jnp.float32), jnp.zeros((HEAD_WIDTH,), jnp.float32), jnp.zeros((HEAD_WIDTH,), jnp.float32))
    inputs = (tokens.reshape(N_FSDP, grouped_rows, MODEL_WIDTH), cotangent.reshape(N_FSDP, grouped_rows, MODEL_WIDTH), seq_lengths)
    sums, (outputs, grads_tok) = lax.scan(group_step, init, inputs)
    g_qkv, g_out, g_gateup, g_down, g_one, g_two, g_q, g_k = sums
    up_qkv = adamw(query_key_value_weight, first_moment_projection, second_moment_projection, g_qkv, MATRIX_RATE, MATRIX_DECAY)
    up_out = adamw(w_out, m_out, v_out, g_out, MATRIX_RATE, MATRIX_DECAY)
    up_gateup = adamw(w_gateup, m_gateup, v_gateup, g_gateup, MATRIX_RATE, MATRIX_DECAY)
    up_down = adamw(w_down, m_down, v_down, g_down, MATRIX_RATE, MATRIX_DECAY)
    up_one = adamw(attn_gain, m_attn_gain, v_attn_gain, g_one, GAIN_RATE, 0.0)
    up_two = adamw(mlp_gain, m_mlp_gain, v_mlp_gain, g_two, GAIN_RATE, 0.0)
    up_q = adamw(q_gain, m_q_gain, v_q_gain, g_q, GAIN_RATE, 0.0)
    up_k = adamw(k_gain, m_k_gain, v_k_gain, g_k, GAIN_RATE, 0.0)
    return (outputs.reshape(N_FSDP * grouped_rows, MODEL_WIDTH), grads_tok.reshape(N_FSDP * grouped_rows, MODEL_WIDTH), g_qkv, up_qkv[0], up_qkv[1], up_qkv[2], g_out, up_out[0], up_out[1], up_out[2], g_gateup, up_gateup[0], up_gateup[1], up_gateup[2], g_down, up_down[0], up_down[1], up_down[2], g_one, up_one[0], up_one[1], up_one[2], g_two, up_two[0], up_two[1], up_two[2], g_q, up_q[0], up_q[1], up_q[2], g_k, up_k[0], up_k[1], up_k[2])
```

```python
import math

import jax
import jax.numpy as jnp
from jax import lax
from jax.experimental import pallas as pl
from jax.experimental.pallas import tpu as pltpu
from jax.sharding import PartitionSpec as P

QUERY_HEADS = 16
KEY_VALUE_HEADS = 8
HEAD_WIDTH = 128
FF = 3072
STEP = 3


NORM_EPS = 1e-06
ROPE_BASE = 1000000.0
NEG_LARGE = -1e30
BETA_ONE = 0.9
BETA_TWO = 0.95
ADAM_EPS = 1e-08
MATRIX_RATE = 0.04
GAIN_RATE = 0.2
MATRIX_DECAY = 0.1


def seq_place(lengths, positions):
    ends = jnp.cumsum(lengths)
    passed = ends[None, :] <= positions[:, None]
    segment = jnp.sum(passed.astype(jnp.int32), axis=1)
    start = jnp.sum(jnp.where(passed, lengths[None, :], 0), axis=1)
    return (segment, positions - start)


def rope_tables(offsets, head_size):
    half_size = head_size // 2
    freqs = ROPE_BASE ** (-(2.0 * jnp.arange(half_size, dtype=jnp.float32)) / head_size)
    angles = offsets.astype(jnp.float32)[:, None] * freqs[None, :]
    cosine = jnp.concatenate([jnp.cos(angles), jnp.cos(angles)], axis=1)[:, None, :]
    sine = jnp.concatenate([jnp.sin(angles), jnp.sin(angles)], axis=1)[:, None, :]
    return (cosine, sine)


def rope_apply(values, cosine, sine):
    half_size = values.shape[-1] // 2
    rotated = jnp.concatenate([-values[..., half_size:], values[..., :half_size]], axis=-1)
    return values * cosine + rotated * sine


def rope_back(grads, cosine, sine):
    half_size = grads.shape[-1] // 2
    scaled = grads * sine
    return grads * cosine + jnp.concatenate(
        [scaled[..., half_size:], -scaled[..., :half_size]], axis=-1
    )


def norm_back(grads, values, inv_rms, gain):
    scaled = grads * gain
    return inv_rms * scaled - values * (inv_rms * inv_rms * inv_rms) * jnp.mean(
        scaled * values, axis=-1, keepdims=True
    )


def adamw(weight, first, second, grads, rate, decay):
    new_first = BETA_ONE * first + (1.0 - BETA_ONE) * grads
    new_second = BETA_TWO * second + (1.0 - BETA_TWO) * grads * grads
    first_hat = new_first / (1.0 - BETA_ONE**STEP)
    second_hat = new_second / (1.0 - BETA_TWO**STEP)
    new_weight = weight - rate * (first_hat / (jnp.sqrt(second_hat) + ADAM_EPS) + decay * weight)
    return (new_weight, new_first, new_second)


def reduce_mlp(grad_gateup, grad_down):
    return (
        lax.psum_scatter(grad_gateup, ("fsdp", "ctx"), scatter_dimension=0, tiled=True),
        lax.psum_scatter(grad_down, ("fsdp", "ctx"), scatter_dimension=0, tiled=True),
    )


def reduce_attn(grad_qkv, grad_out):
    return (
        lax.psum_scatter(grad_qkv, ("fsdp", "ctx"), scatter_dimension=0, tiled=True),
        lax.psum_scatter(grad_out, ("fsdp", "ctx"), scatter_dimension=0, tiled=True),
    )


def plain(
    tokens,
    cotangent,
    seq_lengths,
    query_key_value_weight,
    first_moment_projection,
    second_moment_projection,
    w_out,
    m_out,
    v_out,
    w_gateup,
    m_gateup,
    v_gateup,
    w_down,
    m_down,
    v_down,
    attn_gain,
    m_attn_gain,
    v_attn_gain,
    mlp_gain,
    m_mlp_gain,
    v_mlp_gain,
    q_gain,
    m_q_gain,
    v_q_gain,
    k_gain,
    m_k_gain,
    v_k_gain,
):
    token_rows = tokens.shape[0]
    ctx_index = lax.axis_index("ctx")
    ctx_count = lax.axis_size("ctx")
    reach_back = ctx_count // 2
    rows_in_window = (reach_back + 1) * token_rows
    heads_per_group = QUERY_HEADS // KEY_VALUE_HEADS
    key_value_width = KEY_VALUE_HEADS * HEAD_WIDTH
    score_scale = 1.0 / math.sqrt(HEAD_WIDTH)
    lengths = seq_lengths[0]
    q_places = ctx_index * token_rows + jnp.arange(token_rows, dtype=jnp.int32)
    q_segment, q_offset = seq_place(lengths, q_places)
    k_places = (ctx_index - reach_back) * token_rows + jnp.arange(rows_in_window, dtype=jnp.int32)
    k_segment, k_unused = seq_place(lengths, k_places)
    k_segment = jnp.where(k_places >= 0, k_segment, -1)
    allowed = (q_segment[:, None] == k_segment[None, :]) & (k_places[None, :] <= q_places[:, None])
    cosine, sine = rope_tables(q_offset, HEAD_WIDTH)
    attn_w, out_w = (
        lax.all_gather(
            query_key_value_weight.astype(jnp.bfloat16), ("fsdp", "ctx"), axis=0, tiled=True
        ),
        lax.all_gather(w_out.astype(jnp.bfloat16), ("fsdp", "ctx"), axis=0, tiled=True),
    )
    gateup_w, down_w = (
        lax.all_gather(w_gateup.astype(jnp.bfloat16), ("fsdp", "ctx"), axis=0, tiled=True),
        lax.all_gather(w_down.astype(jnp.bfloat16), ("fsdp", "ctx"), axis=0, tiled=True),
    )
    tok_float = tokens.astype(jnp.float32)
    inv_one = lax.rsqrt(jnp.mean(tok_float * tok_float, axis=1, keepdims=True) + NORM_EPS)
    normed_one = (tok_float * inv_one * attn_gain).astype(jnp.bfloat16)
    projected_rows = jnp.dot(normed_one, attn_w, preferred_element_type=jnp.float32)
    query = projected_rows[:, : QUERY_HEADS * HEAD_WIDTH].reshape(
        token_rows, QUERY_HEADS, HEAD_WIDTH
    )
    unrotated_key = projected_rows[
        :, QUERY_HEADS * HEAD_WIDTH : QUERY_HEADS * HEAD_WIDTH + key_value_width
    ].reshape(token_rows, KEY_VALUE_HEADS, HEAD_WIDTH)
    unprojected_value = projected_rows[:, QUERY_HEADS * HEAD_WIDTH + key_value_width :]
    inv_q = lax.rsqrt(jnp.mean(query * query, axis=2, keepdims=True) + NORM_EPS)
    inv_k = lax.rsqrt(jnp.mean(unrotated_key * unrotated_key, axis=2, keepdims=True) + NORM_EPS)
    rotated_query = rope_apply(query * inv_q * q_gain, cosine, sine).astype(jnp.bfloat16)
    k_rot = rope_apply(unrotated_key * inv_k * k_gain, cosine, sine).astype(jnp.bfloat16)
    kv_own = jnp.concatenate(
        [k_rot.reshape(token_rows, key_value_width), unprojected_value.astype(jnp.bfloat16)], axis=1
    )
    kv_group = lax.all_gather(kv_own, "ctx", axis=0, tiled=True)
    padded = jnp.concatenate(
        [jnp.zeros((reach_back * token_rows, 2 * key_value_width), jnp.bfloat16), kv_group], axis=0
    )
    key_value_window = lax.dynamic_slice_in_dim(padded, ctx_index * token_rows, rows_in_window, 0)
    key_window = key_value_window[:, :key_value_width].reshape(
        rows_in_window, KEY_VALUE_HEADS, HEAD_WIDTH
    )
    value_window = key_value_window[:, key_value_width:].reshape(
        rows_in_window, KEY_VALUE_HEADS, HEAD_WIDTH
    )
    query_four_dims = rotated_query.reshape(
        token_rows, KEY_VALUE_HEADS, heads_per_group, HEAD_WIDTH
    )
    scores = (
        jnp.einsum(
            "tkgd,jkd->kgtj", query_four_dims, key_window, preferred_element_type=jnp.float32
        )
        * score_scale
    )
    scores = jnp.where(allowed, scores, NEG_LARGE)
    peak = jnp.max(scores, axis=3, keepdims=True)
    expd = jnp.exp(scores - peak)
    totals = jnp.sum(expd, axis=3, keepdims=True)
    log_total = peak + jnp.log(totals)
    probs_half = jnp.exp(scores - log_total).astype(jnp.bfloat16)
    attn_half = jnp.einsum(
        "kgtj,jkd->tkgd", probs_half, value_window, preferred_element_type=jnp.float32
    )
    attn_half = attn_half.reshape(token_rows, QUERY_HEADS * HEAD_WIDTH).astype(jnp.bfloat16)
    resid = tok_float + jnp.dot(attn_half, out_w, preferred_element_type=jnp.float32)
    inv_two = lax.rsqrt(jnp.mean(resid * resid, axis=1, keepdims=True) + NORM_EPS)
    normed_two = (resid * inv_two * mlp_gain).astype(jnp.bfloat16)
    gate_up = jnp.dot(normed_two, gateup_w, preferred_element_type=jnp.float32)
    gate = gate_up[:, :FF]
    upper = gate_up[:, FF:]
    sigm = jax.nn.sigmoid(gate)
    active = gate * sigm
    hidden = (active * upper).astype(jnp.bfloat16)
    output = (resid + jnp.dot(hidden, down_w, preferred_element_type=jnp.float32)).astype(
        jnp.bfloat16
    )
    gateup_back, down_back = (
        lax.all_gather(w_gateup.astype(jnp.bfloat16), ("fsdp", "ctx"), axis=0, tiled=True),
        lax.all_gather(w_down.astype(jnp.bfloat16), ("fsdp", "ctx"), axis=0, tiled=True),
    )
    grad_down = jnp.dot(hidden.T, cotangent, preferred_element_type=jnp.float32)
    grad_hidden = jnp.dot(cotangent, down_back.T, preferred_element_type=jnp.float32)
    grad_gate = grad_hidden * upper * (sigm * (1.0 + gate * (1.0 - sigm)))
    grad_upper = grad_hidden * active
    grad_gu = jnp.concatenate([grad_gate, grad_upper], axis=1).astype(jnp.bfloat16)
    grad_gateup = jnp.dot(normed_two.T, grad_gu, preferred_element_type=jnp.float32)
    share_gateup, share_down = reduce_mlp(grad_gateup, grad_down)
    grad_n_two = jnp.dot(grad_gu, gateup_back.T, preferred_element_type=jnp.float32)
    gain_two = jnp.sum(grad_n_two * resid * inv_two, axis=0)
    grad_resid = cotangent.astype(jnp.float32) + norm_back(grad_n_two, resid, inv_two, mlp_gain)
    resid_half = grad_resid.astype(jnp.bfloat16)
    attn_back, out_back = (
        lax.all_gather(
            query_key_value_weight.astype(jnp.bfloat16), ("fsdp", "ctx"), axis=0, tiled=True
        ),
        lax.all_gather(w_out.astype(jnp.bfloat16), ("fsdp", "ctx"), axis=0, tiled=True),
    )
    grad_out = jnp.dot(attn_half.T, resid_half, preferred_element_type=jnp.float32)
    attention_gradient = jnp.dot(resid_half, out_back.T, preferred_element_type=jnp.float32).astype(
        jnp.bfloat16
    )
    attention_gradient = attention_gradient.reshape(
        token_rows, KEY_VALUE_HEADS, heads_per_group, HEAD_WIDTH
    )
    grad_probs = jnp.einsum(
        "tkgd,jkd->kgtj", attention_gradient, value_window, preferred_element_type=jnp.float32
    )
    probs_full = jnp.exp(scores - log_total)
    grad_scores = probs_full * (
        grad_probs - jnp.sum(probs_full * grad_probs, axis=3, keepdims=True)
    )
    scores_half = (grad_scores * score_scale).astype(jnp.bfloat16)
    grad_qrot = jnp.einsum(
        "kgtj,jkd->tkgd", scores_half, key_window, preferred_element_type=jnp.float32
    ).reshape(token_rows, QUERY_HEADS, HEAD_WIDTH)
    grad_kwin = jnp.einsum(
        "kgtj,tkgd->jkd", scores_half, query_four_dims, preferred_element_type=jnp.float32
    ).reshape(rows_in_window, key_value_width)
    grad_vwin = jnp.einsum(
        "kgtj,tkgd->jkd", probs_half, attention_gradient, preferred_element_type=jnp.float32
    ).reshape(rows_in_window, key_value_width)
    grad_window = jnp.concatenate([grad_kwin, grad_vwin], axis=1)
    placed = jnp.zeros(((reach_back + ctx_count) * token_rows, 2 * key_value_width), jnp.float32)
    placed = lax.dynamic_update_slice_in_dim(placed, grad_window, ctx_index * token_rows, 0)
    local_gradient = lax.psum_scatter(
        placed[reach_back * token_rows :].astype(jnp.bfloat16),
        "ctx",
        scatter_dimension=0,
        tiled=True,
    ).astype(jnp.float32)
    rotated_key_gradient = local_gradient[:, :key_value_width].reshape(
        token_rows, KEY_VALUE_HEADS, HEAD_WIDTH
    )
    grad_value = local_gradient[:, key_value_width:]
    grad_qn = rope_back(grad_qrot, cosine, sine)
    grad_kn = rope_back(rotated_key_gradient, cosine, sine)
    gain_q = jnp.sum(grad_qn * query * inv_q, axis=(0, 1))
    gain_k = jnp.sum(grad_kn * unrotated_key * inv_k, axis=(0, 1))
    grad_query = norm_back(grad_qn, query, inv_q, q_gain).reshape(
        token_rows, QUERY_HEADS * HEAD_WIDTH
    )
    grad_key = norm_back(grad_kn, unrotated_key, inv_k, k_gain).reshape(token_rows, key_value_width)
    grad_proj = jnp.concatenate([grad_query, grad_key, grad_value], axis=1).astype(jnp.bfloat16)
    grad_qkv = jnp.dot(normed_one.T, grad_proj, preferred_element_type=jnp.float32)
    grad_n_one = jnp.dot(grad_proj, attn_back.T, preferred_element_type=jnp.float32)
    gain_one = jnp.sum(grad_n_one * tok_float * inv_one, axis=0)
    grad_tokens = grad_resid + norm_back(grad_n_one, tok_float, inv_one, attn_gain)
    share_qkv, share_out = reduce_attn(grad_qkv, grad_out)
    g_one, g_two, g_q, g_k = lax.psum((gain_one, gain_two, gain_q, gain_k), ("fsdp", "ctx"))
    up_qkv = adamw(
        query_key_value_weight,
        first_moment_projection,
        second_moment_projection,
        share_qkv,
        MATRIX_RATE,
        MATRIX_DECAY,
    )
    up_out = adamw(w_out, m_out, v_out, share_out, MATRIX_RATE, MATRIX_DECAY)
    up_gateup = adamw(w_gateup, m_gateup, v_gateup, share_gateup, MATRIX_RATE, MATRIX_DECAY)
    up_down = adamw(w_down, m_down, v_down, share_down, MATRIX_RATE, MATRIX_DECAY)
    up_one = adamw(attn_gain, m_attn_gain, v_attn_gain, g_one, GAIN_RATE, 0.0)
    up_two = adamw(mlp_gain, m_mlp_gain, v_mlp_gain, g_two, GAIN_RATE, 0.0)
    up_q = adamw(q_gain, m_q_gain, v_q_gain, g_q, GAIN_RATE, 0.0)
    up_k = adamw(k_gain, m_k_gain, v_k_gain, g_k, GAIN_RATE, 0.0)
    return (
        output,
        grad_tokens,
        share_qkv,
        up_qkv[0],
        up_qkv[1],
        up_qkv[2],
        share_out,
        up_out[0],
        up_out[1],
        up_out[2],
        share_gateup,
        up_gateup[0],
        up_gateup[1],
        up_gateup[2],
        share_down,
        up_down[0],
        up_down[1],
        up_down[2],
        g_one,
        up_one[0],
        up_one[1],
        up_one[2],
        g_two,
        up_two[0],
        up_two[1],
        up_two[2],
        g_q,
        up_q[0],
        up_q[1],
        up_q[2],
        g_k,
        up_k[0],
        up_k[1],
        up_k[2],
    )


AXES = ("fsdp", "ctx")
CORES = 2
INTERPRET = False


def splits(mesh):
    fsdp, ctx = mesh.shape["fsdp"], mesh.shape["ctx"]
    ring = fsdp // CORES
    return (
        ctx == 2
        and fsdp % CORES == 0
        and ring >= 4
        and ring % 2 == 0
        and KEY_VALUE_HEADS % (ctx * CORES) == 0
        and QUERY_HEADS == ring * CORES
    )


def place():
    index = lax.axis_index("fsdp") * 2 + lax.axis_index("ctx")
    return index // 4, (index // 2) % 2, index % 2


def total_devices():
    return lax.axis_size("fsdp") * 2


def swap_x(value):
    return lax.ppermute(value, AXES, [(i, i ^ 1) for i in range(total_devices())])


def swap_core(value):
    return lax.ppermute(value, AXES, [(i, i ^ 2) for i in range(total_devices())])


def ring_order(count):
    return list(range(0, count, 2)) + list(range(count - 1, 0, -2))


def ring_shift(value, step):
    count = total_devices() // 4
    order = ring_order(count)
    perm = [
        (4 * order[k] + t, 4 * order[(k + step) % count] + t)
        for k in range(count)
        for t in range(4)
    ]
    return lax.ppermute(value, AXES, perm)


def ring_block(spot, distance, count):
    at = (spot + distance + count) % count
    return jnp.where(at < count // 2, 2 * at, 2 * (count - 1 - at) + 1)


def ring_spot(zy, count):
    return jnp.where(zy % 2 == 0, zy // 2, count - 1 - zy // 2)


def pick(value, index, axis):
    return lax.dynamic_index_in_dim(value, index, axis, keepdims=False)


def in_order(own, other, index, axis=0):
    first = jnp.where(index == 0, own, other)
    second = jnp.where(index == 0, other, own)
    return jnp.stack([first, second], axis=axis)


def ring_gather(block, flip):
    count = total_devices() // 4
    zy, _, _ = place()
    spot = ring_spot(zy, count)
    whole = jnp.zeros((count,) + block.shape, block.dtype)
    whole = lax.dynamic_update_index_in_dim(whole, block, zy, 0)
    up = count // 2 if not flip else count - 1 - count // 2
    down = count - 1 - up
    rising, falling = block, block
    for k in range(1, max(up, down) + 1):
        if k <= up:
            rising = ring_shift(rising, 1)
            whole = lax.dynamic_update_index_in_dim(whole, rising, ring_block(spot, -k, count), 0)
        if k <= down:
            falling = ring_shift(falling, -1)
            whole = lax.dynamic_update_index_in_dim(whole, falling, ring_block(spot, k, count), 0)
    return whole.reshape((count * block.shape[0],) + block.shape[1:])


def ring_scatter(grads, flip):
    count = total_devices() // 4
    zy, _, _ = place()
    spot = ring_spot(zy, count)
    blocks = grads.reshape((count, grads.shape[0] // count) + grads.shape[1:])
    up = count // 2 if not flip else count - 1 - count // 2
    down = count - 1 - up

    def term(distance):
        return pick(blocks, ring_block(spot, distance, count), 0)

    def added(got, distance):
        return (got.astype(jnp.float32) + term(distance).astype(jnp.float32)).astype(jnp.bfloat16)

    rising = ring_shift(term(up), 1)
    falling = ring_shift(term(-down), -1)
    for k in range(1, max(up, down)):
        if up - k >= 1:
            rising = ring_shift(added(rising, up - k), 1)
        if down - k >= 1:
            falling = ring_shift(added(falling, -(down - k)), -1)
    return term(0).astype(jnp.float32) + rising.astype(jnp.float32) + falling.astype(jnp.float32)


def spread_columns(pieces):
    _, core, x = place()
    rows, _, width = pieces.shape
    pieces = pieces.reshape(rows, 2, 2, width)
    got = swap_x(pick(pieces, 1 - x, 2))
    both = in_order(pick(pieces, x, 2), got, x)
    got = swap_core(pick(both, 1 - core, 2))
    return in_order(pick(both, core, 2), got, core).reshape(4 * rows, width)


def collect_columns(share):
    _, core, x = place()
    rows, width = share.shape[0] // 4, share.shape[1]
    share = share.reshape(2, 2, rows, width)
    got = swap_x(pick(share, 1 - x, 1))
    both = in_order(pick(share, x, 1), got, x)
    got = swap_core(pick(both, 1 - core, 1))
    four = in_order(pick(both, core, 1), got, core).reshape(4, rows, width)
    return four.transpose(1, 0, 2)


def exchange(pieces):
    _, core, x = place()
    pieces = pieces.reshape((2, 2) + pieces.shape[1:])
    got = swap_x(pick(pieces, 1 - x, 1))
    both = in_order(pick(pieces, x, 1), got, x)
    got = swap_core(pick(both, 1 - core, 1))
    four = in_order(pick(both, core, 1), got, core)
    return four.reshape((4,) + pieces.shape[2:])


def share_rows(value):
    _, core, x = place()
    two = in_order(value, swap_x(value), x)
    four = in_order(two, swap_core(two), core)
    return four.reshape((4 * value.shape[0],) + value.shape[1:])


def core_sum(partial):
    _, core, _ = place()
    halves = partial.reshape((2, partial.shape[0] // 2) + partial.shape[1:])
    got = swap_core(pick(halves, 1 - core, 0).astype(jnp.bfloat16))
    return pick(halves, core, 0) + got.astype(jnp.float32)


def sum_half(partial):
    half = core_sum(partial)
    return half + swap_x(half.astype(jnp.bfloat16)).astype(jnp.float32)


def sum_own(partial):
    _, _, x = place()
    half = core_sum(partial)
    quarters = half.reshape((2, half.shape[0] // 2) + half.shape[1:])
    got = swap_x(pick(quarters, 1 - x, 0).astype(jnp.bfloat16))
    return pick(quarters, x, 0) + got.astype(jnp.float32)


def both_halves(half):
    _, core, _ = place()
    two = in_order(half, swap_core(half), core)
    return two.reshape((2 * half.shape[0],) + half.shape[1:])


def sum_everywhere(value):
    devices = total_devices()
    bit = 1
    while bit < devices:
        value = value + lax.ppermute(value, AXES, [(i, i ^ bit) for i in range(devices)])
        bit *= 2
    return value


def head_norm(raw, gain):
    inverse = lax.rsqrt(jnp.mean(raw * raw, axis=1, keepdims=True) + NORM_EPS)
    return inverse, raw * inverse * gain


def turned(values, cosine, signed):
    half = values.shape[1] // 2
    return values * cosine + pltpu.roll(values, half, 1) * signed


def turned_back(grads, cosine, signed):
    half = grads.shape[1] // 2
    return grads * cosine - pltpu.roll(grads, half, 1) * signed


def dot_t(left, right):
    return lax.dot_general(left, right, (((1,), (1,)), ((), ())), preferred_element_type=jnp.float32)


def t_dot(left, right):
    return lax.dot_general(left, right, (((0,), (0,)), ((), ())), preferred_element_type=jnp.float32)


def softmax_of(query, key, allowed):
    scores = dot_t(query, key) * (1.0 / math.sqrt(HEAD_WIDTH))
    scores = jnp.where(allowed, scores, NEG_LARGE)
    expd = jnp.exp(scores - jnp.max(scores, axis=1, keepdims=True))
    return expd / jnp.sum(expd, axis=1, keepdims=True)


def allowed_of(seg_col_ref, seg_row_ref):
    same = seg_col_ref[...] == seg_row_ref[0]
    rows = lax.broadcasted_iota(jnp.int32, same.shape, 0)
    columns = lax.broadcasted_iota(jnp.int32, same.shape, 1)
    return same & (columns <= rows)


def attend_kernel(
    kv_heads, proj_ref, cos_ref, sin_ref, col_ref, row_ref, q_gain_ref, k_gain_ref, out_ref
):
    per, width = QUERY_HEADS // KEY_VALUE_HEADS, HEAD_WIDTH
    allowed = allowed_of(col_ref, row_ref)
    cosine, signed = cos_ref[...], sin_ref[...]
    k_base, v_base = kv_heads * per * width, kv_heads * (per + 1) * width
    for j in range(kv_heads):
        key = proj_ref[:, k_base + j * width : k_base + (j + 1) * width]
        key = turned(head_norm(key, k_gain_ref[...])[1], cosine, signed).astype(jnp.bfloat16)
        value = proj_ref[:, v_base + j * width : v_base + (j + 1) * width].astype(jnp.bfloat16)
        for h in range(j * per, (j + 1) * per):
            query = proj_ref[:, h * width : (h + 1) * width]
            query = turned(head_norm(query, q_gain_ref[...])[1], cosine, signed)
            probs = softmax_of(query.astype(jnp.bfloat16), key, allowed)
            result = jnp.dot(probs.astype(jnp.bfloat16), value, preferred_element_type=jnp.float32)
            out_ref[:, h * width : (h + 1) * width] = result.astype(jnp.bfloat16)


def attend_back_kernel(
    kv_heads,
    proj_ref,
    grad_ref,
    cos_ref,
    sin_ref,
    col_ref,
    row_ref,
    q_gain_ref,
    k_gain_ref,
    out_ref,
    gains_ref,
):
    per, width = QUERY_HEADS // KEY_VALUE_HEADS, HEAD_WIDTH
    allowed = allowed_of(col_ref, row_ref)
    cosine, signed = cos_ref[...], sin_ref[...]
    q_gain, k_gain = q_gain_ref[...], k_gain_ref[...]
    k_base, v_base = kv_heads * per * width, kv_heads * (per + 1) * width
    q_total = jnp.zeros((1, width), jnp.float32)
    k_total = jnp.zeros((1, width), jnp.float32)

    def through_norm(grads, raw, inverse, gain):
        scaled = grads * gain
        mean = jnp.mean(scaled * raw, axis=1, keepdims=True)
        return inverse * scaled - raw * (inverse * inverse * inverse) * mean

    for j in range(kv_heads):
        k_raw = proj_ref[:, k_base + j * width : k_base + (j + 1) * width]
        k_inverse, k_normed = head_norm(k_raw, k_gain)
        key = turned(k_normed, cosine, signed).astype(jnp.bfloat16)
        value = proj_ref[:, v_base + j * width : v_base + (j + 1) * width].astype(jnp.bfloat16)
        key_grad = jnp.zeros(k_raw.shape, jnp.float32)
        value_grad = jnp.zeros(k_raw.shape, jnp.float32)
        for h in range(j * per, (j + 1) * per):
            raw = proj_ref[:, h * width : (h + 1) * width]
            inverse, normed = head_norm(raw, q_gain)
            query = turned(normed, cosine, signed).astype(jnp.bfloat16)
            probs = softmax_of(query, key, allowed)
            grad = grad_ref[:, h * width : (h + 1) * width]
            probs_grad = dot_t(grad, value)
            inner = jnp.sum(probs * probs_grad, axis=1, keepdims=True)
            scores_grad = probs * (probs_grad - inner) * (1.0 / math.sqrt(HEAD_WIDTH))
            scores_grad = scores_grad.astype(jnp.bfloat16)
            turned_grad = jnp.dot(scores_grad, key, preferred_element_type=jnp.float32)
            key_grad = key_grad + t_dot(scores_grad, query)
            value_grad = value_grad + t_dot(probs.astype(jnp.bfloat16), grad)
            normed_grad = turned_back(turned_grad, cosine, signed)
            q_total = q_total + jnp.sum(normed_grad * raw * inverse, axis=0, keepdims=True)
            result = through_norm(normed_grad, raw, inverse, q_gain)
            out_ref[:, h * width : (h + 1) * width] = result.astype(jnp.bfloat16)
        normed_grad = turned_back(key_grad, cosine, signed)
        k_total = k_total + jnp.sum(normed_grad * k_raw * k_inverse, axis=0, keepdims=True)
        result = through_norm(normed_grad, k_raw, k_inverse, k_gain)
        out_ref[:, k_base + j * width : k_base + (j + 1) * width] = result.astype(jnp.bfloat16)
        out_ref[:, v_base + j * width : v_base + (j + 1) * width] = value_grad.astype(jnp.bfloat16)
    gains_ref[0, 0:1, :] = q_total
    gains_ref[0, 1:2, :] = k_total


def row_specs(rows, width):
    return pl.BlockSpec((rows, width), lambda g: (g, 0))


def fixed_spec(width):
    return pl.BlockSpec((1, width), lambda g: (0, 0))


def attend(kv_heads, rows, proj, tables):
    groups = proj.shape[0] // rows
    width, wide = HEAD_WIDTH, proj.shape[1]
    heads = kv_heads * (QUERY_HEADS // KEY_VALUE_HEADS)
    return pl.pallas_call(
        lambda *refs: attend_kernel(kv_heads, *refs),
        grid=(groups,),
        in_specs=[
            row_specs(rows, wide),
            row_specs(rows, width),
            row_specs(rows, width),
            row_specs(rows, 1),
            pl.BlockSpec((1, 1, rows), lambda g: (g, 0, 0)),
            fixed_spec(width),
            fixed_spec(width),
        ],
        out_specs=row_specs(rows, heads * width),
        out_shape=jax.ShapeDtypeStruct((proj.shape[0], heads * width), jnp.bfloat16),
        cost_estimate=pl.CostEstimate(
            flops=4 * groups * heads * rows * rows * width,
            bytes_accessed=6 * proj.size,
            transcendentals=groups * heads * rows * rows,
        ),
        interpret=INTERPRET,
        name="attend",
    )(proj, *tables)


def attend_back(kv_heads, rows, proj, grad, tables):
    groups = proj.shape[0] // rows
    width, wide = HEAD_WIDTH, proj.shape[1]
    heads = kv_heads * (QUERY_HEADS // KEY_VALUE_HEADS)
    return pl.pallas_call(
        lambda *refs: attend_back_kernel(kv_heads, *refs),
        grid=(groups,),
        in_specs=[
            row_specs(rows, wide),
            row_specs(rows, heads * width),
            row_specs(rows, width),
            row_specs(rows, width),
            row_specs(rows, 1),
            pl.BlockSpec((1, 1, rows), lambda g: (g, 0, 0)),
            fixed_spec(width),
            fixed_spec(width),
        ],
        out_specs=[row_specs(rows, wide), pl.BlockSpec((1, 2, width), lambda g: (g, 0, 0))],
        out_shape=[
            jax.ShapeDtypeStruct(proj.shape, jnp.bfloat16),
            jax.ShapeDtypeStruct((groups, 2, width), jnp.float32),
        ],
        cost_estimate=pl.CostEstimate(
            flops=12 * groups * heads * rows * rows * width,
            bytes_accessed=8 * proj.size,
            transcendentals=groups * heads * rows * rows,
        ),
        interpret=INTERPRET,
        name="attend_back",
    )(proj, grad, *tables)


def mm(left, right):
    return jnp.dot(left, right, preferred_element_type=jnp.float32)


def split_local(
    tokens,
    cotangent,
    seq_lengths,
    query_key_value_weight,
    first_moment_projection,
    second_moment_projection,
    w_out,
    m_out,
    v_out,
    w_gateup,
    m_gateup,
    v_gateup,
    w_down,
    m_down,
    v_down,
    attn_gain,
    m_attn_gain,
    v_attn_gain,
    mlp_gain,
    m_mlp_gain,
    v_mlp_gain,
    q_gain,
    m_q_gain,
    v_q_gain,
    k_gain,
    m_k_gain,
    v_k_gain,
):
    half_type = jnp.bfloat16
    zy, core, x = place()
    ring = total_devices() // 4
    own_rows, model = tokens.shape
    group_rows = 2 * own_rows
    q_cols, kv_cols = QUERY_HEADS * HEAD_WIDTH, KEY_VALUE_HEADS * HEAD_WIDTH
    q_part, kv_part = q_cols // 4, kv_cols // 4
    kv_heads = KEY_VALUE_HEADS // 4
    unit = w_down.shape[0]

    qkv_rows = query_key_value_weight.shape[0]
    half = query_key_value_weight.astype(half_type)
    pieces = jnp.concatenate(
        [
            half[:, :q_cols].reshape(qkv_rows, 4, q_part),
            half[:, q_cols : q_cols + kv_cols].reshape(qkv_rows, 4, kv_part),
            half[:, q_cols + kv_cols :].reshape(qkv_rows, 4, kv_part),
        ],
        axis=2,
    )
    qkv_w = ring_gather(spread_columns(pieces), False)
    out_w = ring_gather(w_out.astype(half_type), True)
    half = w_gateup.astype(half_type).reshape(qkv_rows, 2, ring, 4, unit)
    pieces = half.transpose(0, 3, 1, 2, 4).reshape(qkv_rows, 4, 2 * ring * unit)
    gateup_w = ring_gather(spread_columns(pieces), True)
    down_w = ring_gather(w_down.astype(half_type), False)

    lengths = seq_lengths[0].astype(jnp.float32)
    lengths = in_order(lengths, swap_core(lengths), core).astype(jnp.int32)
    places = jnp.arange(group_rows, dtype=jnp.int32)
    segments, offsets = jax.vmap(lambda row: seq_place(row, places))(lengths)
    freqs = ROPE_BASE ** (
        -(2.0 * jnp.arange(HEAD_WIDTH // 2, dtype=jnp.float32)) / HEAD_WIDTH
    )
    angles = offsets.reshape(-1).astype(jnp.float32)[:, None] * freqs[None, :]
    cosine, sine = jnp.cos(angles), jnp.sin(angles)
    tables = (
        jnp.concatenate([cosine, cosine], axis=1),
        jnp.concatenate([-sine, sine], axis=1),
        segments.reshape(-1, 1),
        segments.reshape(2, 1, group_rows),
        q_gain.reshape(1, -1),
        k_gain.reshape(1, -1),
    )

    tok_all = share_rows(tokens).astype(jnp.float32)
    cot_all = share_rows(cotangent)
    inv_one = lax.rsqrt(jnp.mean(tok_all * tok_all, axis=1, keepdims=True) + NORM_EPS)
    normed_one = (tok_all * inv_one * attn_gain).astype(half_type)
    proj = mm(normed_one, qkv_w)
    attn = attend(kv_heads, group_rows, proj, tables)
    pairs = attn.reshape(4 * own_rows, kv_heads, 2, 2, HEAD_WIDTH // 2)
    pairs = pairs.transpose(2, 3, 0, 1, 4).reshape(4, 4 * own_rows, HEAD_WIDTH)
    attn_mixed = exchange(pairs).transpose(1, 0, 2).reshape(4 * own_rows, 4 * HEAD_WIDTH)
    tok_half = pick(tok_all.reshape(2, group_rows, model), core, 0)
    resid = tok_half + sum_half(mm(attn_mixed, out_w))
    inv_two = lax.rsqrt(jnp.mean(resid * resid, axis=1, keepdims=True) + NORM_EPS)
    normed_two = both_halves((resid * inv_two * mlp_gain).astype(half_type))
    gate_up = mm(normed_two, gateup_w)
    gate, upper = gate_up[:, : ring * unit], gate_up[:, ring * unit :]
    sigm = jax.nn.sigmoid(gate)
    active = gate * sigm
    hidden = (active * upper).astype(half_type)

    grad_down = lax.dot_general(
        hidden, cot_all, (((0,), (0,)), ((), ())), preferred_element_type=jnp.float32
    ).astype(half_type)
    share_down = ring_scatter(grad_down, True)
    grad_hidden = dot_t(cot_all, down_w)
    grad_gate = grad_hidden * upper * (sigm * (1.0 + gate * (1.0 - sigm)))
    grad_upper = grad_hidden * active
    grad_gu = jnp.concatenate([grad_gate, grad_upper], axis=1).astype(half_type)
    grad_gateup = t_dot(normed_two, grad_gu).astype(half_type)
    share_gateup = collect_columns(ring_scatter(grad_gateup, False).astype(half_type))
    share_gateup = share_gateup.reshape(qkv_rows, 4, 2, ring, unit).transpose(0, 2, 3, 1, 4)
    share_gateup = share_gateup.reshape(w_gateup.shape).astype(jnp.float32)
    grad_n_two = sum_half(dot_t(grad_gu, gateup_w))
    own_row = (lax.broadcasted_iota(jnp.int32, (group_rows, 1), 0) // own_rows) == x
    gain_two = jnp.sum(jnp.where(own_row, grad_n_two * resid * inv_two, 0.0), axis=0)
    cot_half = pick(cot_all.reshape(2, group_rows, model), core, 0).astype(jnp.float32)
    grad_resid = cot_half + norm_back(grad_n_two, resid, inv_two, mlp_gain)
    resid_half = both_halves(grad_resid.astype(half_type))
    grad_out = t_dot(attn_mixed, resid_half).astype(half_type)
    share_out = ring_scatter(grad_out, False)
    attn_grad = dot_t(resid_half, out_w).astype(half_type)
    pairs = attn_grad.reshape(4 * own_rows, 4, HEAD_WIDTH).transpose(1, 0, 2)
    pairs = exchange(pairs).reshape(2, 2, 4 * own_rows, kv_heads, HEAD_WIDTH // 2)
    attn_grad = pairs.transpose(2, 3, 0, 1, 4).reshape(4 * own_rows, q_part)
    grad_proj, head_gains = attend_back(kv_heads, group_rows, proj, attn_grad, tables)
    grad_qkv = t_dot(normed_one, grad_proj).astype(half_type)
    share = collect_columns(ring_scatter(grad_qkv, False).astype(half_type)).astype(jnp.float32)
    share_qkv = jnp.concatenate(
        [
            share[:, :, :q_part].reshape(qkv_rows, q_cols),
            share[:, :, q_part : q_part + kv_part].reshape(qkv_rows, kv_cols),
            share[:, :, q_part + kv_part :].reshape(qkv_rows, kv_cols),
        ],
        axis=1,
    )
    grad_n_one = dot_t(grad_proj, qkv_w)
    gain_one = jnp.sum(grad_n_one * tok_all * inv_one, axis=0)
    head_sums = jnp.sum(head_gains, axis=0)
    gains = jnp.concatenate([gain_one, gain_two, head_sums[0], head_sums[1]])
    gains = sum_everywhere(gains.reshape(-1, HEAD_WIDTH)).reshape(-1)
    g_one, g_two = gains[:model], gains[model : 2 * model]
    g_q = gains[2 * model : 2 * model + HEAD_WIDTH]
    g_k = gains[2 * model + HEAD_WIDTH :]

    def own(rows):
        return pick(rows.reshape(2, own_rows, rows.shape[1]), x, 0)

    tok_own = tokens.astype(jnp.float32)
    inv_own = lax.rsqrt(jnp.mean(tok_own * tok_own, axis=1, keepdims=True) + NORM_EPS)
    grad_tokens = own(grad_resid) + norm_back(sum_own(grad_n_one), tok_own, inv_own, attn_gain)
    output = (own(resid) + sum_own(mm(hidden, down_w))).astype(half_type)

    up_qkv = adamw(
        query_key_value_weight,
        first_moment_projection,
        second_moment_projection,
        share_qkv,
        MATRIX_RATE,
        MATRIX_DECAY,
    )
    up_out = adamw(w_out, m_out, v_out, share_out, MATRIX_RATE, MATRIX_DECAY)
    up_gateup = adamw(w_gateup, m_gateup, v_gateup, share_gateup, MATRIX_RATE, MATRIX_DECAY)
    up_down = adamw(w_down, m_down, v_down, share_down, MATRIX_RATE, MATRIX_DECAY)
    up_one = adamw(attn_gain, m_attn_gain, v_attn_gain, g_one, GAIN_RATE, 0.0)
    up_two = adamw(mlp_gain, m_mlp_gain, v_mlp_gain, g_two, GAIN_RATE, 0.0)
    up_q = adamw(q_gain, m_q_gain, v_q_gain, g_q, GAIN_RATE, 0.0)
    up_k = adamw(k_gain, m_k_gain, v_k_gain, g_k, GAIN_RATE, 0.0)
    return (
        output,
        grad_tokens,
        share_qkv,
        *up_qkv,
        share_out,
        *up_out,
        share_gateup,
        *up_gateup,
        share_down,
        *up_down,
        g_one,
        *up_one,
        g_two,
        *up_two,
        g_q,
        *up_q,
        g_k,
        *up_k,
    )


def solution(mesh):
    local = split_local if splits(mesh) else plain
    in_specs = (
        P(("fsdp", "ctx"), None),
        P(("fsdp", "ctx"), None),
        P("fsdp", None),
        P(("fsdp", "ctx"), None),
        P(("fsdp", "ctx"), None),
        P(("fsdp", "ctx"), None),
        P(("fsdp", "ctx"), None),
        P(("fsdp", "ctx"), None),
        P(("fsdp", "ctx"), None),
        P(("fsdp", "ctx"), None),
        P(("fsdp", "ctx"), None),
        P(("fsdp", "ctx"), None),
        P(("fsdp", "ctx"), None),
        P(("fsdp", "ctx"), None),
        P(("fsdp", "ctx"), None),
        P(),
        P(),
        P(),
        P(),
        P(),
        P(),
        P(),
        P(),
        P(),
        P(),
        P(),
        P(),
    )
    out_specs = (
        P(("fsdp", "ctx"), None),
        P(("fsdp", "ctx"), None),
        P(("fsdp", "ctx"), None),
        P(("fsdp", "ctx"), None),
        P(("fsdp", "ctx"), None),
        P(("fsdp", "ctx"), None),
        P(("fsdp", "ctx"), None),
        P(("fsdp", "ctx"), None),
        P(("fsdp", "ctx"), None),
        P(("fsdp", "ctx"), None),
        P(("fsdp", "ctx"), None),
        P(("fsdp", "ctx"), None),
        P(("fsdp", "ctx"), None),
        P(("fsdp", "ctx"), None),
        P(("fsdp", "ctx"), None),
        P(("fsdp", "ctx"), None),
        P(("fsdp", "ctx"), None),
        P(("fsdp", "ctx"), None),
        P(),
        P(),
        P(),
        P(),
        P(),
        P(),
        P(),
        P(),
        P(),
        P(),
        P(),
        P(),
        P(),
        P(),
        P(),
        P(),
    )
    return jax.shard_map(local, mesh=mesh, in_specs=in_specs, out_specs=out_specs, check_vma=False)
```
